32 devices in a mesh: seq: 8 (over z, y), tp: 4 (over x, core).
Axes of the slice: x: 2, y: 2, z: 4, core: 2. Of those that a mesh axis runs over, the one named last changes fastest.
Arguments:
- block_input: bfloat16 [6144, 1024], P('seq'), may hold values from -6 to 6
- seq_starts: int32 [6144], P('seq'), may hold values from 0 to 1, as said below
- norm_scale_one: float32 [1024], replicated, may hold values from 0.5 to 1.5
- in_proj: bfloat16 [1024, 3, 1024], P(None, None, 'tp'), may hold values from -0.1875 to 0.1875
- conv_kernel: float32 [3, 1024], P(None, 'tp'), may hold values from -3 to 3
- out_proj: bfloat16 [1024, 1024], P('tp'), may hold values from -0.1875 to 0.1875
- norm_scale_two: float32 [1024], replicated, may hold values from 0.5 to 1.5
- gate_up_proj: bfloat16 [1024, 2, 4608], P(None, None, 'tp'), may hold values from -0.1875 to 0.1875
- down_proj: bfloat16 [4608, 1024], P('tp'), may hold values from -0.1875 to 0.1875
- out_cotangent: bfloat16 [6144, 1024], P('seq'), may hold values from -6 to 6
Outputs:
- block_output: bfloat16 [6144, 1024], P(('seq', 'tp'))
- input_grad: float32 [6144, 1024], P(('seq', 'tp'))
- in_proj_grad: float32 [1024, 3, 1024], P('seq', None, 'tp')
- conv_kernel_grad: float32 [3, 1024], P(None, 'tp')
- out_proj_grad: float32 [1024, 1024], P('tp', 'seq')
- gate_up_grad: float32 [1024, 2, 4608], P('seq', None, 'tp')
- down_proj_grad: float32 [4608, 1024], P('tp', 'seq')
- norm_scale_one_grad: float32 [1024], P('tp')
- norm_scale_two_grad: float32 [1024], P('tp')
The draws below stay inside these ranges and needn't reach their ends.
Inputs may be any that keep to these rules, and one draw needn't show every extreme that they name: `seq_starts`: exactly two entries are 1: token 0, and token k * 768 - 1 for some k with 1 <= k < 8, the last token of a device's block.
All inputs are finite; a program needn't handle non-finite values.
Results may differ from the reference program's by a relative error of at most 0.014.
Values may be sent and summed in bfloat16 or wider, within the bound.
No kernel may reach another device: no remote copies, remote signals or barrier semaphores. Data moves between devices by JAX's collectives and lax.ppermute only.
A program may use at most 192 MiB of HBM per device.

```python
import math
import jax
import jax.numpy as jnp
from jax import lax

D = 1024
FF = 4608
KERNEL = 3
TOK_DEV = 768
TOKENS = 6144


def draw_seq_starts(key, part):
    block_pick = jax.random.randint(key, (1,), 1, TOKENS // TOK_DEV)
    second = block_pick[0] * TOK_DEV - 1
    places = jnp.arange(TOKENS, dtype=jnp.int32)
    return ((places == 0) | (places == second)).astype(jnp.int32)


def strengthened(entries, key, source, target, blocks, factor):
    owner, partner = [(jnp.arange(entries.shape[axis_at]) // (entries.shape[axis_at] // blocks)).reshape([-1 if axis == axis_at else 1 for axis in range(entries.ndim)]) for axis_at in (source, target)]
    chosen = jax.random.permutation(key, blocks)[partner]
    strong = (owner == chosen) | (owner == (partner + blocks // 2) % blocks)
    return jnp.where(strong, factor * entries, entries)


def steps_of(own_key, extent, cuts, smallest, top_value):
    level = 1.0
    for axis_at, shards_of in cuts:
        draws = jax.random.uniform(jax.random.fold_in(jax.random.fold_in(own_key, 6), axis_at), (shards_of,), jnp.float32, smallest / len(cuts), top_value / len(cuts))
        level = level * jnp.repeat(jnp.exp(draws), extent[axis_at] // shards_of).reshape((-1,) + (1,) * (len(extent) - 1 - axis_at))
    return level


def gaussian(key, extent, spread, most, cuts=(), kind=jnp.bfloat16):
    array = jax.random.normal(key, extent, jnp.float32) * spread
    if len(cuts) > 0:
        array = steps_of(key, extent, cuts, -0.22, 0.18) * array
    return jnp.clip(array, min=-most, max=most).astype(kind)


def gaussian_with(own_key, shape, deviation, limit, pieces, heavy, held_as=jnp.bfloat16):
    array = deviation * jax.random.normal(own_key, shape, jnp.float32)
    if pieces:
        array = array * steps_of(own_key, shape, pieces, -0.22, 0.18)
    return jnp.clip(strengthened(array, jax.random.fold_in(own_key, 3), *heavy), -limit, limit).astype(held_as)


def setup_inputs(seed: int = 0) -> dict:
    seeds = jax.random.split(jax.random.key(seed), 11)
    block_input = gaussian_with(seeds[0], (TOKENS, D), 1.0, 6.0, ((0, 8),), (0, 1, 8, 2.0))
    seq_starts = draw_seq_starts(jax.random.fold_in(seeds[10], 71), 0)
    norm_scale_one = jnp.clip(1.0 + 0.1 * jax.random.normal(seeds[2], (D,), jnp.float32), 0.5, 1.5)
    in_proj = gaussian(seeds[3], (D, 3, D), D ** -0.5, 0.1875, ((2, 4),))
    conv_kernel = gaussian(seeds[4], (KERNEL, D), 0.6, 3.0, ((1, 4),), jnp.float32)
    out_proj = gaussian(seeds[5], (D, D), D ** -0.5, 0.1875, ((0, 4),))
    norm_scale_two = jnp.clip(1.0 + 0.1 * jax.random.normal(seeds[6], (D,), jnp.float32), 0.5, 1.5)
    gate_up_proj = gaussian(seeds[7], (D, 2, FF), D ** -0.5, 0.1875, ((2, 4),))
    down_proj = gaussian(seeds[8], (FF, D), (FF // 4) ** -0.5, 0.1875, ((0, 4),))
    out_cotangent = gaussian_with(seeds[9], (TOKENS, D), 1.0, 6.0, ((0, 8),), (0, 1, 8, 2.0))
    return {"block_input": block_input, "seq_starts": seq_starts, "norm_scale_one": norm_scale_one, "in_proj": in_proj, "conv_kernel": conv_kernel, "out_proj": out_proj, "norm_scale_two": norm_scale_two, "gate_up_proj": gate_up_proj, "down_proj": down_proj, "out_cotangent": out_cotangent}


EPS = 1e-05

def inverse_rms(values):
    return lax.rsqrt(lax.optimization_barrier(jnp.mean(values * values, -1, keepdims=True)) + EPS)

def norm_back(grad_normed, source, inverse, scale_vec):
    weighted = grad_normed * scale_vec
    return inverse * (weighted - source * inverse * inverse * lax.optimization_barrier(jnp.mean(weighted * source, -1, keepdims=True)))

def inner_rows(left, right):
    return lax.dot_general(left, right, (((0,), (0,)), ((), ())), preferred_element_type=jnp.float32)

def outer_cols(left, right):
    return lax.dot_general(left, right, (((1,), (1,)), ((), ())), preferred_element_type=jnp.float32)

def ffn_block(normed_two, cotangent, gate_up_flat, down_proj):
    units = down_proj.shape[0]
    both_vals = jnp.dot(normed_two, gate_up_flat, preferred_element_type=jnp.float32)
    gate_val = both_vals[:, :units]
    up_val = both_vals[:, units:]
    sigmoid_g = jax.nn.sigmoid(gate_val)
    activ = (gate_val * sigmoid_g * up_val).astype(jnp.bfloat16)
    ffn_out = jnp.dot(activ, down_proj, preferred_element_type=jnp.float32)
    d_activ = outer_cols(cotangent, down_proj)
    d_up = d_activ * gate_val * sigmoid_g
    d_gate = d_activ * up_val * sigmoid_g * (1.0 + gate_val * (1.0 - sigmoid_g))
    d_both = jnp.concatenate([d_gate, d_up], 1).astype(jnp.bfloat16)
    d_normed = outer_cols(d_both, gate_up_flat)
    return (ffn_out, d_normed, inner_rows(normed_two, d_both), inner_rows(activ, cotangent))

def reference(block_input, seq_starts, norm_scale_one, in_proj, conv_kernel, out_proj, norm_scale_two, gate_up_proj, down_proj, out_cotangent):
    model_width = block_input.shape[1]
    float_in = block_input.astype(jnp.float32)
    scale_one = inverse_rms(float_in)
    normed_one = (float_in * scale_one * norm_scale_one).astype(jnp.bfloat16)
    in_flat = in_proj.reshape(model_width, 3 * model_width)
    projected = jnp.dot(normed_one, in_flat, preferred_element_type=jnp.float32)
    b_part = projected[:, :model_width]
    c_part = projected[:, model_width:2 * model_width]
    x_part = projected[:, 2 * model_width:]
    product_bx = (b_part * x_part).astype(jnp.bfloat16)
    starts = seq_starts.astype(jnp.float32)[:, None]
    keep_one = 1.0 - starts
    keep_two = keep_one * (1.0 - jnp.concatenate([jnp.zeros((1, 1), jnp.float32), starts[:-1]]))
    padded = jnp.concatenate([jnp.zeros((2, model_width), jnp.float32), product_bx.astype(jnp.float32)])
    conv_out = conv_kernel[0] * padded[2:] + keep_one * conv_kernel[1] * padded[1:-1] + keep_two * conv_kernel[2] * padded[:-2]
    gated = (c_part * conv_out).astype(jnp.bfloat16)
    resid = float_in + jnp.dot(gated, out_proj, preferred_element_type=jnp.float32)
    scale_two = inverse_rms(resid)
    normed_two = (resid * scale_two * norm_scale_two).astype(jnp.bfloat16)
    block_rows = math.gcd(TOKENS, 4096)
    count_blocks = TOKENS // block_rows
    gate_up_flat = gate_up_proj.reshape(model_width, 2 * FF)

    def ffn_step(carry, inputs):
        ffn_out, d_normed, grad_gu_part, grad_down_part = ffn_block(inputs[0], inputs[1], gate_up_flat, down_proj)
        return ((carry[0] + grad_gu_part, carry[1] + grad_down_part), (ffn_out, d_normed))
    start_grads = (jnp.zeros((model_width, 2 * FF), jnp.float32), jnp.zeros((FF, model_width), jnp.float32))
    blocks_in = (normed_two.reshape(count_blocks, block_rows, model_width), out_cotangent.reshape(count_blocks, block_rows, model_width))
    (grad_gu, grad_down), (ffn_all, d_normed_two) = lax.scan(ffn_step, start_grads, blocks_in)
    ffn_all = ffn_all.reshape(TOKENS, model_width)
    d_normed_two = d_normed_two.reshape(TOKENS, model_width)
    block_output = (resid + ffn_all).astype(jnp.bfloat16)
    d_resid = out_cotangent.astype(jnp.float32) + norm_back(d_normed_two, resid, scale_two, norm_scale_two)
    grad_scale_two = lax.optimization_barrier(jnp.sum(d_normed_two * resid * scale_two, 0))
    d_resid_b = d_resid.astype(jnp.bfloat16)
    d_gated = outer_cols(d_resid_b, out_proj)
    grad_out = inner_rows(gated, d_resid_b)
    d_c = d_gated * conv_out
    d_conv = d_gated * c_part
    e_one = d_conv * keep_one
    e_two = d_conv * keep_two
    d_prod = conv_kernel[0] * d_conv
    d_prod = d_prod + conv_kernel[1] * jnp.concatenate([e_one[1:], jnp.zeros((1, model_width), jnp.float32)])
    d_prod = d_prod + conv_kernel[2] * jnp.concatenate([e_two[2:], jnp.zeros((2, model_width), jnp.float32)])
    grad_kernel = jnp.stack([lax.optimization_barrier(jnp.sum(d_conv * padded[2:], 0)), lax.optimization_barrier(jnp.sum(e_one * padded[1:-1], 0)), lax.optimization_barrier(jnp.sum(e_two * padded[:-2], 0))])
    d_proj = jnp.concatenate([d_prod * x_part, d_c, d_prod * b_part], 1).astype(jnp.bfloat16)
    grad_in = inner_rows(normed_one, d_proj).reshape(model_width, 3, model_width)
    d_normed_one = outer_cols(d_proj, in_flat)
    input_grad = d_resid + norm_back(d_normed_one, float_in, scale_one, norm_scale_one)
    grad_scale_one = lax.optimization_barrier(jnp.sum(d_normed_one * float_in * scale_one, 0))
    return (block_output, input_grad, grad_in, grad_kernel, grad_out, grad_gu.reshape(model_width, 2, FF), grad_down, grad_scale_one, grad_scale_two)
```

```python
import jax
import jax.numpy as jnp
from jax import lax
from jax.sharding import PartitionSpec as P

EPS = 1e-05
BF = jnp.bfloat16
F32 = jnp.float32


def bits_of(axis):
    size = lax.axis_size(axis)
    count = size.bit_length() - 1
    assert size == 1 << count
    return tuple(1 << k for k in range(count))


def swap(value, axis, bit):
    peers = lax.axis_size(axis)
    return lax.ppermute(value, axis, [(i, i ^ bit) for i in range(peers)])


def shifted(shard, axis, by):
    peers = lax.axis_size(axis)
    pairs = [(i, i + by) for i in range(peers) if 0 <= i + by < peers]
    return lax.ppermute(shard, axis, pairs)


def inverse_rms(values):
    return lax.rsqrt(jnp.mean(values * values, -1, keepdims=True) + EPS)


def norm_back(grad_normed, source, inverse, scale_vec):
    weighted = grad_normed * scale_vec
    return inverse * (
        weighted - source * inverse * inverse * jnp.mean(weighted * source, -1, keepdims=True)
    )


def inner_rows(left, right):
    return lax.dot_general(
        left, right, (((0,), (0,)), ((), ())), preferred_element_type=F32
    )


def outer_cols(left, right):
    return lax.dot_general(
        left, right, (((1,), (1,)), ((), ())), preferred_element_type=F32
    )


def dot(left, right):
    return jnp.dot(left, right, preferred_element_type=F32)


def halving_order(bits):
    order = [0]
    for bit in reversed(bits):
        order = order + [r ^ bit for r in order]
    return order


def relative_cols(values, axis, bits):
    me = lax.axis_index(axis)
    width = values.shape[1] // lax.axis_size(axis)
    return jnp.concatenate(
        [
            lax.dynamic_slice_in_dim(values, (me ^ r) * width, width, 1)
            for r in halving_order(bits)
        ],
        1,
    )


def scatter_seq(grads, bits):
    current = grads
    for bit in bits:
        half = current.shape[0] // 2
        arrived = swap(current[half:].astype(BF), "seq", bit)
        current = current[:half].astype(F32) + arrived.astype(F32)
    return current


def gather_tp(own):
    parts = [own]
    for bit in reversed(bits_of("tp")):
        parts = parts + [swap(part, "tp", bit) for part in parts]
    return parts


def gather_index():
    order = [0]
    for bit in reversed(bits_of("tp")):
        order = order + [r ^ bit for r in order]
    return order


def scatter_tp(partial):
    me = lax.axis_index("tp")
    share = partial.shape[0] // lax.axis_size("tp")

    def block(r):
        return lax.dynamic_slice_in_dim(partial, (me ^ r) * share, share, 0)

    bits = bits_of("tp")
    order = halving_order(bits)
    blocks = [block(r) for r in order]
    for bit in bits:
        half = len(blocks) // 2
        sent = jnp.concatenate([b.astype(BF) for b in blocks[half:]])
        arrived = swap(sent, "tp", bit).astype(F32)
        blocks = [
            blocks[i] + arrived[i * share : (i + 1) * share] for i in range(half)
        ]
    return blocks[0]


def body(
    block_input,
    seq_starts,
    norm_scale_one,
    in_proj,
    conv_kernel,
    out_proj,
    norm_scale_two,
    gate_up_proj,
    down_proj,
    out_cotangent,
):
    rows_all = block_input.shape[0]
    model_width = block_input.shape[1]
    channels = in_proj.shape[2]
    units = down_proj.shape[0]
    tp_devices = lax.axis_size("tp")
    row_share = rows_all // tp_devices
    tp_me = lax.axis_index("tp")
    row_start = tp_me * row_share
    chan_start = tp_me * channels
    seq_bits = bits_of("seq")
    z_first = seq_bits[1:] + seq_bits[:1]

    def share_of(values):
        return lax.dynamic_slice_in_dim(values, row_start, row_share, 0)

    starts = seq_starts.astype(F32)[:, None]
    keep_one = 1.0 - starts
    keep_two = keep_one * (1.0 - jnp.concatenate([jnp.zeros((1, 1), F32), starts[:-1]]))
    rim_mask = jnp.concatenate([1.0 - starts[-1:], jnp.ones((1, 1), F32)])
    tail_rows = (block_input[-2:].astype(F32) * rim_mask).astype(BF)
    incoming = shifted(tail_rows, "seq", 1)
    out_parts = gather_tp(out_proj)

    float_in = block_input.astype(F32)
    scale_one = inverse_rms(float_in)
    normed_one = (float_in * scale_one * norm_scale_one).astype(BF)
    in_flat = in_proj.reshape(model_width, 3 * channels)
    projected = dot(normed_one, in_flat)
    b_part = projected[:, :channels]
    c_part = projected[:, channels : 2 * channels]
    x_part = projected[:, 2 * channels :]
    product_bx = (b_part * x_part).astype(BF)
    halo_in = jnp.concatenate([jnp.zeros((6, model_width), F32), incoming.astype(F32)])
    halo_normed = (halo_in * inverse_rms(halo_in) * norm_scale_one).astype(BF)
    halo_proj = dot(halo_normed, in_flat)
    halo_bx = (halo_proj[-2:, :channels] * halo_proj[-2:, 2 * channels :]).astype(BF)
    padded = jnp.concatenate([halo_bx, product_bx]).astype(F32)
    conv_out = (
        conv_kernel[0] * padded[2:]
        + keep_one * conv_kernel[1] * padded[1:-1]
        + keep_two * conv_kernel[2] * padded[:-2]
    )
    gated = (c_part * conv_out).astype(BF)
    gated_parts = gather_tp(gated)

    d_activ = outer_cols(out_cotangent, down_proj)
    cotangent_rel = relative_cols(out_cotangent, "seq", z_first)
    normed_one_rel = relative_cols(normed_one, "seq", seq_bits)

    resid = float_in
    for left, right in zip(gated_parts, out_parts):
        resid = resid + dot(left, right)
    scale_two = inverse_rms(resid)
    normed_two = (resid * scale_two * norm_scale_two).astype(BF)
    gate_w = gate_up_proj[:, 0, :]
    up_w = gate_up_proj[:, 1, :]
    gate_val = dot(normed_two, gate_w)
    up_val = dot(normed_two, up_w)
    sigmoid_g = jax.nn.sigmoid(gate_val)
    activ = (gate_val * sigmoid_g * up_val).astype(BF)
    d_up = (d_activ * gate_val * sigmoid_g).astype(BF)
    d_gate = (d_activ * up_val * sigmoid_g * (1.0 + gate_val * (1.0 - sigmoid_g))).astype(BF)

    d_normed_part = outer_cols(d_gate, gate_w) + outer_cols(d_up, up_w)
    d_normed_share = scatter_tp(d_normed_part)
    resid_share = share_of(resid)
    scale_two_share = share_of(scale_two)
    d_resid_share = share_of(out_cotangent).astype(F32) + norm_back(
        d_normed_share, resid_share, scale_two_share, norm_scale_two
    )
    grad_scale_two = jnp.sum(d_normed_share * resid_share * scale_two_share, 0)

    down_total = scatter_seq(inner_rows(cotangent_rel, activ).astype(BF), z_first).T
    normed_two_rel = relative_cols(normed_two, "seq", seq_bits)
    gate_total = scatter_seq(inner_rows(normed_two_rel, d_gate).astype(BF), seq_bits)
    up_total = scatter_seq(inner_rows(normed_two_rel, d_up).astype(BF), seq_bits)
    ffn_share = scatter_tp(dot(activ, down_proj))
    output_share = (resid_share + ffn_share).astype(BF)

    resid_b_parts = jnp.stack(gather_tp(d_resid_share.astype(BF)))
    place = gather_index()
    d_resid_b = jnp.concatenate(
        [
            lax.dynamic_index_in_dim(
                resid_b_parts, jnp.asarray([place.index(r) for r in range(tp_devices)])[tp_me ^ j], 0, False
            )
            for j in range(tp_devices)
        ]
    )
    d_gated = outer_cols(d_resid_b, out_proj)
    out_total = scatter_seq(
        inner_rows(relative_cols(d_resid_b, "seq", seq_bits), gated).astype(BF), seq_bits
    ).T
    d_c = d_gated * conv_out
    d_conv = d_gated * c_part
    e_one = d_conv * keep_one
    e_two = d_conv * keep_two
    back_rim = jnp.concatenate(
        [conv_kernel[2] * e_two[:1], conv_kernel[1] * e_one[:1] + conv_kernel[2] * e_two[1:2]]
    )
    arriving = shifted(back_rim, "seq", -1) * rim_mask
    d_prod = conv_kernel[0] * d_conv
    d_prod = d_prod + conv_kernel[1] * jnp.concatenate([e_one[1:], jnp.zeros((1, channels), F32)])
    d_prod = d_prod + conv_kernel[2] * jnp.concatenate([e_two[2:], jnp.zeros((2, channels), F32)])
    d_prod = d_prod + jnp.concatenate([jnp.zeros((rows_all - 2, channels), F32), arriving])
    grad_kernel = jnp.stack(
        [
            jnp.sum(d_conv * padded[2:], 0),
            jnp.sum(e_one * padded[1:-1], 0),
            jnp.sum(e_two * padded[:-2], 0),
        ]
    )
    d_proj = jnp.concatenate([d_prod * x_part, d_c, d_prod * b_part], 1).astype(BF)
    d_one_part = outer_cols(d_proj, in_flat)
    d_one_share = scatter_tp(d_one_part)
    in_total = scatter_seq(inner_rows(normed_one_rel, d_proj).astype(BF), seq_bits)
    float_share = share_of(float_in)
    scale_one_share = share_of(scale_one)
    input_grad = d_resid_share + norm_back(
        d_one_share, float_share, scale_one_share, norm_scale_one
    )
    grad_scale_one = jnp.sum(d_one_part * float_in * scale_one, 0)

    small = jnp.concatenate(
        [
            lax.dynamic_update_slice(
                jnp.zeros((3, model_width), F32), grad_kernel, (0, chan_start)
            ),
            jnp.stack([grad_scale_one, grad_scale_two]),
            jnp.zeros((3, model_width), F32),
        ]
    )
    for axis in ("tp", "seq"):
        for bit in bits_of(axis):
            small = small + swap(small, axis, bit)
    small_mine = lax.dynamic_slice_in_dim(small, chan_start, channels, 1)
    gain_cols = model_width // tp_devices
    gains_mine = lax.dynamic_slice_in_dim(small[3:5], tp_me * gain_cols, gain_cols, 1)
    return (
        output_share,
        input_grad,
        in_total.reshape(in_total.shape[0], 3, channels),
        small_mine[:3],
        out_total,
        jnp.stack([gate_total, up_total], 1),
        down_total,
        gains_mine[0],
        gains_mine[1],
    )


def solution(mesh):
    in_specs = (
        P("seq", None),
        P("seq"),
        P(),
        P(None, None, "tp"),
        P(None, "tp"),
        P("tp", None),
        P(),
        P(None, None, "tp"),
        P("tp", None),
        P("seq", None),
    )
    out_specs = (
        P(("seq", "tp"), None),
        P(("seq", "tp"), None),
        P("seq", None, "tp"),
        P(None, "tp"),
        P("tp", "seq"),
        P("seq", None, "tp"),
        P("tp", "seq"),
        P("tp"),
        P("tp"),
    )
    return jax.shard_map(body, mesh=mesh, in_specs=in_specs, out_specs=out_specs, check_vma=False)
```
